32 devices in a mesh: rep: 4 (over y, x), ep: 8 (over z, core).
Axes of the slice: x: 2, y: 2, z: 4, core: 2. Of those that a mesh axis runs over, the one named last changes fastest.
Arguments:
- tokens: bfloat16 [8192, 768], P(('rep', 'ep')), may hold values from -6 to 6
- segment_ids: int32 [4, 2048], P('rep', 'ep'), may hold values from 0 to 3, never falling along the last dimension, each value on 1 to 1024 neighbouring positions
- routes: int32 [8192, 2], P(('rep', 'ep')), may hold values from 0 to 7, all different within a row; in each aligned block of 256 rows (0 to 255, 256 to 511, ...) at most 128 rows name the same one
- norm1_gain: bfloat16 [768], P(('rep', 'ep')), may hold values from 0.5 to 1.5
- w_query: bfloat16 [768, 768], P(('rep', 'ep')), may hold values from -0.3125 to 0.3125
- w_key: bfloat16 [768, 768], P(('rep', 'ep')), may hold values from -0.3125 to 0.3125
- w_value: bfloat16 [768, 768], P(('rep', 'ep')), may hold values from -0.21875 to 0.21875
- w_out: bfloat16 [768, 768], P(('rep', 'ep')), may hold values from -1.25 to 1.25
- norm2_gain: bfloat16 [768], P(('rep', 'ep')), may hold values from 0.5 to 1.5
- w_router: bfloat16 [768, 8], P(('rep', 'ep')), may hold values from -0.15625 to 0.15625
- shared_gate: bfloat16 [768, 2048], P(('rep', 'ep')), may hold values from -0.21875 to 0.21875
- shared_up: bfloat16 [768, 2048], P(('rep', 'ep')), may hold values from -0.21875 to 0.21875
- shared_down: bfloat16 [2048, 768], P(('rep', 'ep')), may hold values from -0.1875 to 0.1875
- expert_gate: bfloat16 [8, 768, 2048], P('ep'), may hold values from -0.21875 to 0.21875
- expert_up: bfloat16 [8, 768, 2048], P('ep'), may hold values from -0.21875 to 0.21875
- expert_down: bfloat16 [8, 2048, 768], P('ep'), may hold values from -1.5 to 1.5
- out_grad: bfloat16 [8192, 768], P(('rep', 'ep')), may hold values from -6 to 6
Outputs:
- layer_out: bfloat16 [8192, 768], P(('rep', 'ep'))
- tokens_grad: float32 [8192, 768], P(('rep', 'ep'))
- norm1_gain_grad: float32 [768], P(('rep', 'ep'))
- w_query_grad: float32 [768, 768], P(('rep', 'ep'))
- w_key_grad: float32 [768, 768], P(('rep', 'ep'))
- w_value_grad: float32 [768, 768], P(('rep', 'ep'))
- w_out_grad: float32 [768, 768], P(('rep', 'ep'))
- norm2_gain_grad: float32 [768], P(('rep', 'ep'))
- w_router_grad: float32 [768, 8], P(('rep', 'ep'))
- shared_gate_grad: float32 [768, 2048], P(('rep', 'ep'))
- shared_up_grad: float32 [768, 2048], P(('rep', 'ep'))
- shared_down_grad: float32 [2048, 768], P(('rep', 'ep'))
- expert_gate_grad: float32 [8, 768, 2048], P('ep', None, 'rep')
- expert_up_grad: float32 [8, 768, 2048], P('ep', None, 'rep')
- expert_down_grad: float32 [8, 2048, 768], P('ep', None, 'rep')
The draws below stay inside these ranges and needn't reach their ends.
Inputs may be any that keep to these rules, and one draw needn't show every extreme that they name: `segment_ids`: along each pack of 2048 places the document number never falls; every document has 1 to 1024 places, and one has exactly 1024. `routes`: each token names 2 different experts. Among the 256 tokens of one device no expert is named more than 128 times, and in some device's tokens one expert is named exactly 128 times.
All inputs are finite; a program needn't handle non-finite values.
Results may differ from the reference program's by a relative error of at most 0.03.
Values may be sent and summed in bfloat16 or wider, within the bound.
No kernel may reach another device: no remote copies, remote signals or barrier semaphores. Data moves between devices by JAX's collectives and lax.ppermute only.
A program may use at most 256 MiB of HBM per device.

```python
import math
import jax
import jax.numpy as jnp
import numpy as np
from jax import lax

D = 768
HEADS = 12
HEAD_DIM = 64
FF = 2048
TOPK = 2
BLOCK = 256
TOK_DEV = 256
EXPERTS = 8
ROW_LEN = 2048
SEQ_MAX = 1024
DOCS = 4
CAP = 128
PACKS = 4
TOKENS = 8192
N_REP = 4
N_EP = 8


def raised(values, rng, source, target, parts, factor):
    owner, partner = [(jnp.arange(values.shape[dim]) // (values.shape[dim] // parts)).reshape([-1 if axis == dim else 1 for axis in range(values.ndim)]) for dim in (source, target)]
    chosen = jax.random.permutation(rng, parts)[partner]
    strong = (owner == chosen) | (owner == (partner + parts // 2) % parts)
    return jnp.where(strong, factor * values, values)


def levels(key, dims, shards, smallest, top_value):
    level = 1.0
    for dim, blocks in shards:
        draws = jax.random.uniform(jax.random.fold_in(jax.random.fold_in(key, 6), dim), (blocks,), jnp.float32, smallest / len(shards), top_value / len(shards))
        level = level * jnp.repeat(jnp.exp(draws), dims[dim] // blocks).reshape((-1,) + (1,) * (len(dims) - 1 - dim))
    return level


def length_profile(count, total, limit, slope):
    loads = [(1 << 20) // math.isqrt(standing ** slope) + 1 for standing in range(2, count + 1)]
    rest, given = total - limit - (count - 1), [1] * (count - 1)
    while rest > 0:
        free = [i for i in range(count - 1) if given[i] < limit]
        whole, remaining = sum([loads[i] for i in free]), rest
        for i in free:
            extra = min(limit - given[i], max(1, remaining * loads[i] // whole), rest)
            given[i] = given[i] + extra
            rest = rest - extra
    return np.array([limit] + given)


def uneven_parts(rng, number_of, total, bound, slope):
    if number_of == 2:
        one = jax.random.randint(rng, (), max(1, total - bound), min(bound, total - 1) + 1)
        return jnp.stack([one, total - one])
    lengths = jnp.asarray(length_profile(number_of, total, bound, slope), jnp.int32)
    twos = (number_of - 1) // 2
    donor, taker = lengths[1:1 + 2 * twos:2], lengths[2:2 + 2 * twos:2]
    room = jnp.minimum(donor - 1, bound - taker)
    moved = jax.random.randint(jax.random.fold_in(rng, 1), (twos,), 0, 1 << 20) % (room + 1)
    lengths = lengths.at[1:1 + 2 * twos:2].set(donor - moved).at[2:2 + 2 * twos:2].set(taker + moved)
    return lengths[jax.random.permutation(jax.random.fold_in(rng, 2), number_of)]


def deal_out(key, own, number, rows, count, top, reach, skew):
    order = jax.random.permutation(key, count)
    heavy_load, usual = load_shares(count, rows * top, reach, skew, True), load_shares(count, rows * top, reach, skew, False)
    places = jnp.arange(count)

    def named(sizes, turn):
        used = int((sizes > 0).sum())
        fixed = max(1, used // 4)
        moved = fixed + (places - fixed + turn * (used - fixed)) % max(1, count - fixed)
        return jnp.zeros((count,), jnp.int32).at[order[jnp.where(places < fixed, places, moved)]].set(jnp.asarray(sizes, jnp.int32))

    sizes = jnp.where(number % 4 == 0, named(heavy_load, number // 4), named(usual, number - number // 4 - 1))
    mixed = jax.random.permutation(jax.random.fold_in(own, 3), count)
    source_of, sink = mixed[0:count // 2 * 2:2], mixed[1:count // 2 * 2:2]
    room = jnp.minimum(sizes[source_of] - 1, reach - sizes[sink]) // 2
    room = jnp.where((source_of == order[0]) | (sink == order[0]) | (sizes[sink] == 0), 0, jnp.maximum(room, 0))
    moved = jax.random.randint(jax.random.fold_in(own, 4), (count // 2,), 0, 1 << 20) % (room + 1)
    sizes = sizes.at[source_of].add(-moved).at[sink].add(moved)
    members = jnp.searchsorted(jnp.cumsum(sizes), jnp.arange(rows * top), side="right").astype(jnp.int32)
    grid = members.reshape(top, rows).T
    grid = grid[jax.random.permutation(jax.random.fold_in(own, 1), rows)]
    turn = jax.random.randint(jax.random.fold_in(own, 2), (rows, 1), 0, top)
    return jnp.take_along_axis(grid, (jnp.arange(top)[None, :] + turn) % top, axis=1)


def load_shares(count, total, most, slope, full):
    portions = [(1 << 20) // math.isqrt(grade ** slope) + 1 for grade in range(1, count + 1)]
    largest = most if full else min(most, max(-(-total // count), total * portions[0] // sum(portions)))
    least = 1 if total - largest >= count - 1 else 0
    holding, rest = [largest] + [least] * (count - 1), total - largest - least * (count - 1)
    while rest > 0:
        movable = [i for i in range(1, count) if holding[i] < largest] or [i for i in range(1, count) if holding[i] < most]
        pool, left = sum([portions[i] for i in movable]), rest
        for i in movable:
            more = min(most - holding[i], max(1, left * portions[i] // pool), rest)
            holding[i] = holding[i] + more
            rest = rest - more
    return np.array(holding)


def normal_values(stream_key, dims, deviation, bound, cuts=(), kind=jnp.bfloat16):
    values = deviation * jax.random.normal(stream_key, dims, jnp.float32)
    if cuts:
        values = values * levels(stream_key, dims, cuts, -0.22, 0.18)
    return jnp.clip(values, -bound, bound).astype(kind)


def heavy_noise(rng, shape, spread, limit, cuts, heavy, kind=jnp.bfloat16):
    values = spread * jax.random.normal(rng, shape, jnp.float32)
    if cuts:
        values = values * levels(rng, shape, cuts, -0.22, 0.18)
    return jnp.clip(raised(values, jax.random.fold_in(rng, 3), *heavy), -limit, limit).astype(kind)


def setup_inputs(seed: int = 0) -> dict:
    splits = jax.random.split(jax.random.key(seed), 18)
    tokens = normal_values(splits[0], (TOKENS, D), 1.0, 6.0, ((0, 32),))
    segment_ids = jax.vmap(lambda own: jnp.searchsorted(jnp.cumsum(uneven_parts(own, DOCS, ROW_LEN, SEQ_MAX, 1)), jnp.arange(ROW_LEN), side="right"))(jax.random.split(splits[1], PACKS)).reshape((PACKS, ROW_LEN)).astype(jnp.int32)
    routes_keys = jax.random.split(jax.random.fold_in(splits[2], 1), TOKENS // TOK_DEV)
    routes_turns = jax.random.permutation(jax.random.fold_in(splits[2], 3), TOKENS // TOK_DEV)
    routes = jax.vmap(lambda own, number: deal_out(jax.random.fold_in(splits[2], 2), own, number, TOK_DEV, EXPERTS, TOPK, CAP, 2))(routes_keys, routes_turns).reshape((TOKENS, TOPK))
    norm1_gain = jnp.clip(1.0 + 0.1 * jax.random.normal(splits[3], (D,), jnp.float32), 0.5, 1.5).astype(jnp.bfloat16)
    w_query = normal_values(splits[4], (D, D), (D // 2) ** -0.5, 0.3125, ((0, 32),))
    w_key = normal_values(splits[5], (D, D), (D // 2) ** -0.5, 0.3125, ((0, 32),))
    w_value = normal_values(splits[6], (D, D), D ** -0.5, 0.21875, ((0, 32),))
    w_out = normal_values(splits[7], (D, D), (D // 32) ** -0.5, 1.25, ((0, 32),))
    norm2_gain = jnp.clip(1.0 + 0.1 * jax.random.normal(splits[8], (D,), jnp.float32), 0.5, 1.5).astype(jnp.bfloat16)
    w_router = normal_values(splits[9], (D, EXPERTS), (2 * D) ** -0.5, 0.15625, ((0, 32),))
    shared_gate = normal_values(splits[10], (D, FF), D ** -0.5, 0.21875, ((0, 32),))
    shared_up = normal_values(splits[11], (D, FF), D ** -0.5, 0.21875, ((0, 32),))
    shared_down = normal_values(splits[12], (FF, D), (FF // 2) ** -0.5, 0.1875, ((0, 32),))
    expert_gate = normal_values(splits[13], (EXPERTS, D, FF), D ** -0.5, 0.21875, ((0, 8),))
    expert_up = normal_values(splits[14], (EXPERTS, D, FF), D ** -0.5, 0.21875, ((0, 8),))
    expert_down = normal_values(splits[15], (EXPERTS, FF, D), (FF // 128) ** -0.5, 1.5, ((0, 8),))
    out_grad = heavy_noise(splits[16], (TOKENS, D), 1.0, 6.0, ((0, 32),), (0, 1, 32, 2.75))
    return {"tokens": tokens, "segment_ids": segment_ids, "routes": routes, "norm1_gain": norm1_gain, "w_query": w_query, "w_key": w_key, "w_value": w_value, "w_out": w_out, "norm2_gain": norm2_gain, "w_router": w_router, "shared_gate": shared_gate, "shared_up": shared_up, "shared_down": shared_down, "expert_gate": expert_gate, "expert_up": expert_up, "expert_down": expert_down, "out_grad": out_grad}


@jax.custom_vjp
def low(v):
    return lax.optimization_barrier(v.astype(jnp.bfloat16)).astype(jnp.float32)

@jax.custom_vjp
def low_back(v):
    return v

def low_keep(v):
    return (low(v), None)

def low_pass(kept, grad):
    return (grad,)

def back_keep(v):
    return (v, None)

def back_low(kept, grad):
    return (low(grad),)
low.defvjp(low_keep, low_pass)
low_back.defvjp(back_keep, back_low)
EPSILON = 1e-06
NEG_LARGE = -1e+30
HIGHEST_MODE = lax.Precision.HIGHEST

def precise(former, latter):
    return jnp.dot(former, latter, precision=HIGHEST_MODE, preferred_element_type=jnp.float32)

def rms_scale(values):
    return lax.rsqrt(lax.optimization_barrier(jnp.mean(values * values, axis=1, keepdims=True)) + EPSILON)

def silu_value(values):
    return values * jax.nn.sigmoid(values)

def rotate(values, cosine_table, sine_table):
    halfway = values.shape[-1] // 2
    front_half = values[..., :halfway]
    back_half = values[..., halfway:]
    return jnp.concatenate([front_half * cosine_table - back_half * sine_table, back_half * cosine_table + front_half * sine_table], axis=-1)

def turn_tables(places, head_dim):
    halfway = head_dim // 2
    inverse = jnp.exp(jnp.arange(halfway).astype(jnp.float32) * (-2.0 * math.log(10000.0) / head_dim))
    turned = places.astype(jnp.float32)[:, None] * inverse[None, :]
    return (jnp.cos(turned)[:, None, :], jnp.sin(turned)[:, None, :])

def reference(tokens, segment_ids, routes, norm1_gain, w_query, w_key, w_value, w_out, norm2_gain, w_router, shared_gate, shared_up, shared_down, expert_gate, expert_up, expert_down, out_grad):
    choice_count = TOKENS * TOPK
    expert_room = CAP * N_REP * N_EP
    flat_routes = routes.reshape(choice_count).astype(jnp.int32)
    onehot = (flat_routes[:, None] == jnp.arange(EXPERTS, dtype=jnp.int32)[None, :]).astype(jnp.int32)
    own_rank = lax.optimization_barrier(jnp.sum((jnp.cumsum(onehot, axis=0) - 1) * onehot, axis=1)).astype(jnp.int32)
    slot_of_choice = (flat_routes * expert_room + own_rank).astype(jnp.int32)
    slot_source = jnp.full((EXPERTS * expert_room,), choice_count, jnp.int32).at[slot_of_choice].set(jnp.arange(choice_count, dtype=jnp.int32))
    slot_token_row = jnp.where(slot_source < choice_count, slot_source // TOPK, TOKENS).astype(jnp.int32).reshape(EXPERTS, expert_room)
    places = (jnp.arange(TOKENS, dtype=jnp.int32) % ROW_LEN).astype(jnp.int32)
    cosine_table, sine_table = turn_tables(places, HEAD_DIM)
    route_table = (routes[:, :, None] == jnp.arange(EXPERTS, dtype=jnp.int32)[None, None, :]).astype(jnp.float32)
    segments = segment_ids.reshape(PACKS, ROW_LEN)
    step_rows = math.gcd(ROW_LEN, 512)
    score_scale = HEAD_DIM ** (-0.5)

    def attend_pack(packed):
        pack_queries, pack_keys, pack_values, pack_segments = packed
        key_places = jnp.arange(ROW_LEN, dtype=jnp.int32)

        def attend_block(block_index):
            offset = block_index * step_rows
            block_queries = lax.dynamic_slice_in_dim(pack_queries, offset, step_rows, 0)
            block_segments = lax.dynamic_slice_in_dim(pack_segments, offset, step_rows, 0)
            query_places = offset + jnp.arange(step_rows, dtype=jnp.int32)
            allowed = jnp.logical_and(block_segments[:, None] == pack_segments[None, :], key_places[None, :] // BLOCK <= query_places[:, None] // BLOCK)[None]
            scores = low_back(jnp.einsum('qhd,khd->hqk', block_queries, pack_keys, precision=HIGHEST_MODE) * score_scale)
            scores = jnp.where(allowed, scores, NEG_LARGE)
            shifted = jnp.exp(scores - lax.optimization_barrier(jnp.max(scores, axis=2, keepdims=True)))
            weights = shifted / lax.optimization_barrier(jnp.sum(shifted, axis=2, keepdims=True))
            return jnp.einsum('hqk,khd->qhd', low(weights), pack_values, precision=HIGHEST_MODE)
        blocks = lax.map(jax.checkpoint(attend_block), jnp.arange(ROW_LEN // step_rows, dtype=jnp.int32))
        return blocks.reshape(ROW_LEN, HEADS, HEAD_DIM)

    def forward_pass(layer_inputs, first_norm_gain, query_matrix, key_matrix, value_matrix, output_matrix, second_norm_gain, router_matrix, shared_gate_matrix, shared_up_matrix, shared_down_matrix, expert_gate_matrix, expert_up_matrix, expert_down_matrix):
        normed_one = layer_inputs * rms_scale(layer_inputs)
        hidden_one = low(normed_one * first_norm_gain)
        query_raw = low_back(precise(hidden_one, query_matrix)).reshape(TOKENS, HEADS, HEAD_DIM)
        queries = low(rotate(query_raw, cosine_table, sine_table))
        key_raw = low_back(precise(hidden_one, key_matrix)).reshape(TOKENS, HEADS, HEAD_DIM)
        keys_all = low(rotate(key_raw, cosine_table, sine_table))
        values_all = low(low_back(precise(hidden_one, value_matrix))).reshape(TOKENS, HEADS, HEAD_DIM)
        attended = lax.map(attend_pack, (queries.reshape(PACKS, ROW_LEN, HEADS, HEAD_DIM), keys_all.reshape(PACKS, ROW_LEN, HEADS, HEAD_DIM), values_all.reshape(PACKS, ROW_LEN, HEADS, HEAD_DIM), segments))
        attended_low = low(low_back(attended.reshape(TOKENS, D)))
        middle = layer_inputs + low_back(precise(attended_low, output_matrix))
        normed_two = middle * rms_scale(middle)
        hidden_two = low(normed_two * second_norm_gain)
        logits = low_back(precise(hidden_two, router_matrix))
        shifted = jnp.exp(logits - lax.optimization_barrier(jnp.max(logits, axis=1, keepdims=True)))
        router_probs = shifted / lax.optimization_barrier(jnp.sum(shifted, axis=1, keepdims=True))
        gate_values = lax.optimization_barrier(jnp.sum(router_probs[:, None, :] * route_table, axis=2))
        shared_pre = low_back(precise(hidden_two, shared_gate_matrix))
        shared_lin = low_back(precise(hidden_two, shared_up_matrix))
        shared_hidden = low(silu_value(shared_pre) * shared_lin)
        shared_result = precise(shared_hidden, shared_down_matrix)
        padded_rows = jnp.concatenate([hidden_two, jnp.zeros((1, D), jnp.float32)], axis=0)

        def expert_layer_block(packed):
            gate_weight, up_weight, down_weight, row_index = packed
            routed_rows = low_back(padded_rows[row_index])
            gate_pre = low_back(precise(routed_rows, gate_weight))
            up_pre = low_back(precise(routed_rows, up_weight))
            expert_hidden = low(silu_value(gate_pre) * up_pre)
            return low(low_back(precise(expert_hidden, down_weight)))
        expert_outputs = lax.map(jax.checkpoint(expert_layer_block), (expert_gate_matrix, expert_up_matrix, expert_down_matrix, slot_token_row))
        picked = expert_outputs.reshape(EXPERTS * expert_room, D)[slot_of_choice].reshape(TOKENS, TOPK, D)
        mixture = lax.optimization_barrier(jnp.sum(gate_values[:, :, None] * picked, axis=1))
        return middle + shared_result + mixture
    float_args = (tokens.astype(jnp.float32), norm1_gain.astype(jnp.float32), w_query.astype(jnp.float32), w_key.astype(jnp.float32), w_value.astype(jnp.float32), w_out.astype(jnp.float32), norm2_gain.astype(jnp.float32), w_router.astype(jnp.float32), shared_gate.astype(jnp.float32), shared_up.astype(jnp.float32), shared_down.astype(jnp.float32), expert_gate.astype(jnp.float32), expert_up.astype(jnp.float32), expert_down.astype(jnp.float32))
    result, pullback = jax.vjp(forward_pass, *float_args)
    gradients = pullback(out_grad.astype(jnp.float32))
    return (result.astype(jnp.bfloat16), gradients[0], gradients[1], gradients[2], gradients[3], gradients[4], gradients[5], gradients[6], gradients[7], gradients[8], gradients[9], gradients[10], gradients[11], gradients[12], gradients[13])
```

```python
import math

import jax
import jax.numpy as jnp
from jax import lax
from jax.experimental import pallas as pl
from jax.experimental.pallas import tpu as pltpu
from jax.sharding import PartitionSpec as P

HEADS = 12
HEAD_DIM = 64
SLAB = 2 * HEAD_DIM
EPSILON = 1e-06
NEG_LARGE = -1e30
BF = jnp.bfloat16
F32 = jnp.float32
ALL = ("rep", "ep")


def dot(a, b):
    return lax.dot_general(a, b, (((1,), (0,)), ((), ())), preferred_element_type=F32)


def dot_nt(a, b):
    return lax.dot_general(a, b, (((1,), (1,)), ((), ())), preferred_element_type=F32)


def dot_tn(a, b):
    return lax.dot_general(a, b, (((0,), (0,)), ((), ())), preferred_element_type=F32)


def rms_scale(values):
    return lax.rsqrt(jnp.mean(values * values, axis=1, keepdims=True) + EPSILON)


def swap_halves(values):
    width = values.shape[1]
    half = HEAD_DIM // 2
    lane = lax.broadcasted_iota(jnp.int32, values.shape, 1)
    return jnp.where(
        lane % HEAD_DIM < half,
        pltpu.roll(values, width - half, 1),
        pltpu.roll(values, half, 1),
    )


def head_mask(rows, head):
    lane = lax.broadcasted_iota(jnp.int32, (rows, SLAB), 1)
    return jnp.where(lane // HEAD_DIM == head, 1.0, 0.0).astype(BF)


def project_kernel(x_ref, w_ref, g_ref, cos_ref, sin_ref, h_ref, k_ref, v_ref, q_ref):
    width = x_ref.shape[1]
    x = x_ref[...].astype(F32)
    hidden = (x * rms_scale(x) * g_ref[...]).astype(BF)
    h_ref[...] = hidden
    copies = width // SLAB
    cos = jnp.concatenate([cos_ref[...]] * copies, axis=1)
    sin = jnp.concatenate([sin_ref[...]] * copies, axis=1)
    key = dot(hidden, w_ref[:, width : 2 * width])
    k_ref[...] = (key * cos + swap_halves(key) * sin).astype(BF)
    v_ref[...] = dot(hidden, w_ref[:, 2 * width : 3 * width]).astype(BF)

    @pl.when(pl.program_id(0) == 0)
    def _():
        query = dot(hidden, w_ref[:, :width])
        q_ref[...] = (query * cos + swap_halves(query) * sin).astype(BF)


def project(x_win, weights, gain, cos, sin, rows):
    total, width = x_win.shape
    return pl.pallas_call(
        project_kernel,
        grid=(total // rows,),
        in_specs=[
            pl.BlockSpec((rows, width), lambda i: (i, 0)),
            pl.BlockSpec((width, 3 * width), lambda i: (0, 0)),
            pl.BlockSpec((1, width), lambda i: (0, 0)),
            pl.BlockSpec((rows, SLAB), lambda i: (i, 0)),
            pl.BlockSpec((rows, SLAB), lambda i: (i, 0)),
        ],
        out_specs=[
            pl.BlockSpec((rows, width), lambda i: (i, 0)),
            pl.BlockSpec((rows, width), lambda i: (i, 0)),
            pl.BlockSpec((rows, width), lambda i: (i, 0)),
            pl.BlockSpec((rows, width), lambda i: (0, 0)),
        ],
        out_shape=[jax.ShapeDtypeStruct((total, width), BF)] * 3
        + [jax.ShapeDtypeStruct((rows, width), BF)],
        name="project",
    )(x_win, weights, gain, cos, sin)


def attend_kernel(
    near_ref, q_ref, k_ref, v_ref, sq_ref, sk_ref, o_ref, l_ref, s_buf, m_buf, d_buf, a_buf
):
    rows = q_ref.shape[0]
    slots = k_ref.shape[0] // rows
    scale = HEAD_DIM**-0.5
    seg_q = sq_ref[...]
    lane = lax.broadcasted_iota(jnp.int32, (rows, SLAB), 1)
    parts = []
    for head in range(2):
        query = q_ref[...] * head_mask(rows, head)
        m_buf[...] = jnp.full_like(m_buf, NEG_LARGE)
        d_buf[...] = jnp.zeros_like(d_buf)
        a_buf[...] = jnp.zeros_like(a_buf)
        for j in range(slots):

            @pl.when(near_ref[j] > 0)
            def _(j=j, query=query):
                scores = dot_nt(query, k_ref[j * rows : (j + 1) * rows, :]) * scale
                scores = jnp.where(seg_q == sk_ref[j], scores, NEG_LARGE)
                s_buf[j] = scores
                top = m_buf[...]
                for n in range(rows // SLAB):
                    top = jnp.maximum(top, scores[:, n * SLAB : (n + 1) * SLAB])
                m_buf[...] = top

        top = jnp.max(m_buf[...], axis=1, keepdims=True)
        for j in range(slots):

            @pl.when(near_ref[j] > 0)
            def _(j=j, top=top):
                probs = jnp.exp(s_buf[j] - top)
                total = d_buf[...]
                for n in range(rows // SLAB):
                    total = total + probs[:, n * SLAB : (n + 1) * SLAB]
                d_buf[...] = total
                a_buf[...] += dot(probs.astype(BF), v_ref[j * rows : (j + 1) * rows, :])

        total = jnp.sum(d_buf[...], axis=1, keepdims=True)
        parts.append((a_buf[...] / total, top + jnp.log(total)))
    first = lane < HEAD_DIM
    o_ref[...] = jnp.where(first, parts[0][0], parts[1][0])
    l_ref[...] = jnp.where(first, parts[0][1], parts[1][1])


def attend(near, q, k, v, seg_q, seg_k):
    rows, width = q.shape
    total = k.shape[0]
    slots = total // rows
    grid_spec = pltpu.PrefetchScalarGridSpec(
        num_scalar_prefetch=1,
        grid=(width // SLAB,),
        in_specs=[
            pl.BlockSpec((rows, SLAB), lambda i, n: (0, i)),
            pl.BlockSpec((total, SLAB), lambda i, n: (0, i)),
            pl.BlockSpec((total, SLAB), lambda i, n: (0, i)),
            pl.BlockSpec((rows, 1), lambda i, n: (0, 0)),
            pl.BlockSpec((slots, 1, rows), lambda i, n: (0, 0, 0)),
        ],
        out_specs=[
            pl.BlockSpec((rows, SLAB), lambda i, n: (0, i)),
            pl.BlockSpec((rows, SLAB), lambda i, n: (0, i)),
        ],
        scratch_shapes=[
            pltpu.VMEM((slots, rows, rows), F32),
            pltpu.VMEM((rows, SLAB), F32),
            pltpu.VMEM((rows, SLAB), F32),
            pltpu.VMEM((rows, SLAB), F32),
        ],
    )
    return pl.pallas_call(
        attend_kernel,
        grid_spec=grid_spec,
        out_shape=[jax.ShapeDtypeStruct((rows, width), F32)] * 2,
        name="attend",
    )(near, q, k, v, seg_q[:, None], seg_k.reshape(slots, 1, rows))


def attend_back_kernel(
    near_ref,
    q_ref,
    k_ref,
    v_ref,
    g_ref,
    o_ref,
    l_ref,
    sq_ref,
    sk_ref,
    cos_ref,
    sin_ref,
    dq_ref,
    dk_ref,
    dv_ref,
    acc,
):
    rows = q_ref.shape[0]
    slots = k_ref.shape[0] // rows
    scale = HEAD_DIM**-0.5
    grads = g_ref[...]
    masks = [head_mask(rows, head) for head in range(2)]
    q_cat = jnp.concatenate([q_ref[...] * m for m in masks], axis=0)
    g_cat = jnp.concatenate([grads * m for m in masks], axis=0)
    lse_t = jnp.transpose(l_ref[...])
    delta_t = jnp.transpose(grads.astype(F32) * o_ref[...])
    lse = jnp.concatenate([lse_t[:1], lse_t[HEAD_DIM : HEAD_DIM + 1]], axis=1)
    delta = jnp.concatenate(
        [
            jnp.sum(delta_t[:HEAD_DIM], axis=0, keepdims=True),
            jnp.sum(delta_t[HEAD_DIM:], axis=0, keepdims=True),
        ],
        axis=1,
    )
    seg_q = jnp.concatenate([sq_ref[...]] * 2, axis=1)
    acc[...] = jnp.zeros_like(acc)

    def turned(values, cos, sin):
        values = values * scale
        return (values * cos - swap_halves(values) * sin).astype(BF)

    for j in range(slots):
        part = slice(j * rows, (j + 1) * rows)

        @pl.when(near_ref[j] > 0)
        def _(part=part):
            keys = k_ref[part, :]
            scores = dot_nt(keys, q_cat) * scale
            probs = jnp.where(sk_ref[part, :] == seg_q, jnp.exp(scores - lse), 0.0)
            prob_grads = dot_nt(v_ref[part, :], g_cat)
            score_grads = (probs * (prob_grads - delta)).astype(BF)
            dk = dot(score_grads, q_cat)
            dk_ref[part, :] = turned(dk, cos_ref[part, :], sin_ref[part, :])
            dv_ref[part, :] = dot(probs.astype(BF), g_cat).astype(BF)
            acc[...] += dot_tn(score_grads[:, :rows], keys * masks[0]) + dot_tn(
                score_grads[:, rows:], keys * masks[1]
            )

        @pl.when(near_ref[j] <= 0)
        def _(part=part):
            dk_ref[part, :] = jnp.zeros((rows, SLAB), BF)
            dv_ref[part, :] = jnp.zeros((rows, SLAB), BF)

    dq_ref[...] = turned(acc[...], cos_ref[:rows, :], sin_ref[:rows, :])


def attend_back(near, q, k, v, grads, attended, lse, seg_q, seg_k, cos, sin):
    rows, width = q.shape
    total = k.shape[0]
    own = pl.BlockSpec((rows, SLAB), lambda i, n: (0, i))
    window = pl.BlockSpec((total, SLAB), lambda i, n: (0, i))
    table = pl.BlockSpec((total, SLAB), lambda i, n: (0, 0))
    grid_spec = pltpu.PrefetchScalarGridSpec(
        num_scalar_prefetch=1,
        grid=(width // SLAB,),
        in_specs=[
            own,
            window,
            window,
            own,
            own,
            own,
            pl.BlockSpec((1, rows), lambda i, n: (0, 0)),
            pl.BlockSpec((total, 1), lambda i, n: (0, 0)),
            table,
            table,
        ],
        out_specs=[own, window, window],
        scratch_shapes=[pltpu.VMEM((rows, SLAB), F32)],
    )
    return pl.pallas_call(
        attend_back_kernel,
        grid_spec=grid_spec,
        out_shape=[
            jax.ShapeDtypeStruct((rows, width), BF),
            jax.ShapeDtypeStruct((total, width), BF),
            jax.ShapeDtypeStruct((total, width), BF),
        ],
        name="attend_back",
    )(near, q, k, v, grads, attended, lse, seg_q[None, :], seg_k[:, None], cos, sin)


def shards(
    tokens,
    segment_ids,
    routes,
    norm1_gain,
    w_query,
    w_key,
    w_value,
    w_out,
    norm2_gain,
    w_router,
    shared_gate,
    shared_up,
    shared_down,
    expert_gate,
    expert_up,
    expert_down,
    out_grad,
):
    rows, width = tokens.shape
    reps = lax.axis_size("rep")
    group = lax.axis_size("ep")
    place = lax.axis_index("ep")
    pack_rows = rows * group
    top_count = routes.shape[1]
    experts = w_router.shape[1]
    capacity = 2 * rows * top_count // experts
    ff = shared_gate.shape[1]
    ff_part = ff // group
    ff_row = ff_part // reps
    pad = SLAB

    swap = [(i, i ^ 1) for i in range(group)]
    upward = [(i, i + 2) for i in range(group - 2)]
    downward = [(i + 2, i) for i in range(group - 2)]
    back = group // 4

    small = jnp.concatenate(
        [
            norm1_gain[:, None],
            norm2_gain[:, None],
            w_router,
            jnp.zeros((w_router.shape[0], pad - 2 - experts), BF),
        ],
        axis=1,
    )
    dense = lax.all_gather(
        jnp.concatenate([w_query, w_key, w_value, w_out, small], axis=1), ALL, axis=0, tiled=True
    )
    meta = lax.all_gather(
        jnp.concatenate([segment_ids.reshape(1, rows), routes.T], axis=0), "ep", axis=0
    )
    seg_all = meta[:, 0, :]
    slots = [tokens, lax.ppermute(tokens, "ep", swap)]
    current = tokens
    for _ in range(back):
        current = lax.ppermute(current, "ep", upward)
        slots += [current, lax.ppermute(current, "ep", swap)]
    x_win = jnp.concatenate(slots, axis=0)
    block_of_slot = jnp.stack(
        [base - 2 * k for k in range(back + 1) for base in (place, place ^ 1)]
    )
    seg_own = segment_ids.reshape(rows)
    usable = jnp.logical_and(block_of_slot >= 0, block_of_slot <= place)
    seg_win = jnp.where(usable[:, None], seg_all[jnp.clip(block_of_slot, 0, group - 1)], -1)
    near = (jnp.max(seg_win, axis=1) >= seg_own[0]).astype(jnp.int32)
    seg_win = seg_win.reshape(-1)

    half = HEAD_DIM // 2
    inverse = jnp.exp(jnp.arange(half).astype(F32) * (-2.0 * math.log(10000.0) / HEAD_DIM))
    places = (block_of_slot[:, None] * rows + jnp.arange(rows, dtype=jnp.int32)).reshape(-1)
    turned = places.astype(F32)[:, None] * inverse[None, :]
    cos, sin = jnp.cos(turned), jnp.sin(turned)
    cos = jnp.concatenate([cos] * 4, axis=1)
    sin = jnp.concatenate([-sin, sin] * 2, axis=1)

    grad_all = lax.all_gather(out_grad, "ep", axis=0, tiled=True)

    pieces = jnp.concatenate(
        [
            shared_gate.reshape(-1, reps, group, ff_row).transpose(2, 0, 1, 3).reshape(
                group, -1, ff_part
            ),
            shared_up.reshape(-1, reps, group, ff_row).transpose(2, 0, 1, 3).reshape(
                group, -1, ff_part
            ),
        ],
        axis=2,
    )
    pieces = lax.all_to_all(pieces, "ep", split_axis=0, concat_axis=0, tiled=True)
    shared_in = lax.all_gather(pieces, "rep", axis=0, tiled=True).reshape(width, 2 * ff_part)
    gate_part = shared_in[:, :ff_part]
    up_part = shared_in[:, ff_part:]
    down_part = lax.all_gather(shared_down, "rep", axis=0, tiled=True)

    gain_first = dense[:, 4 * width].astype(F32)[None, :]
    gain_second = dense[:, 4 * width + 1].astype(F32)[None, :]
    router = dense[:, 4 * width + 2 : 4 * width + 2 + experts]
    output_matrix = dense[:, 3 * width : 4 * width]
    hidden_win, k_win, v_win, queries = project(x_win, dense, gain_first, cos, sin, rows)
    attended, lse = attend(near, queries, k_win, v_win, seg_own, seg_win)
    attended_low = attended.astype(BF)
    layer_inputs = tokens.astype(F32)
    middle = layer_inputs + dot(attended_low, output_matrix)
    scale_second = rms_scale(middle)
    normed_second = middle * scale_second
    hidden_second = (normed_second * gain_second).astype(BF)

    hidden_all = lax.all_gather(hidden_second, "ep", axis=0, tiled=True)

    chosen = jnp.any(meta[:, 1:, :] == place, axis=1)
    chosen_low = chosen.astype(BF)
    before = (
        lax.broadcasted_iota(jnp.int32, (rows, rows), 0)
        < lax.broadcasted_iota(jnp.int32, (rows, rows), 1)
    ).astype(BF)
    rank = dot(chosen_low, before)
    picker = jnp.where(
        jnp.logical_and(
            chosen[:, None, :],
            rank[:, None, :] == jnp.arange(capacity, dtype=jnp.int32).astype(F32)[None, :, None],
        ),
        1.0,
        0.0,
    ).astype(BF)

    def pick(values):
        return lax.dot_general(
            picker,
            values.reshape(group, rows, -1),
            (((2,), (1,)), ((0,), (0,))),
            preferred_element_type=F32,
        ).reshape(group * capacity, -1)

    def unpick(values):
        return lax.dot_general(
            picker,
            values.reshape(group, capacity, -1),
            (((1,), (1,)), ((0,), (0,))),
            preferred_element_type=F32,
        ).reshape(pack_rows, -1)

    gate_matrix, up_matrix, down_matrix = expert_gate[0], expert_up[0], expert_down[0]
    grads_in = pick(grad_all).astype(BF)
    hidden_grad_raw = dot_nt(grads_in, down_matrix)
    shared_hidden_grad = dot_nt(grad_all, down_part)

    logits = dot(hidden_all, router)
    shifted = jnp.exp(logits - jnp.max(logits, axis=1, keepdims=True))
    router_probs = shifted / jnp.sum(shifted, axis=1, keepdims=True)
    own_column = lax.broadcasted_iota(jnp.int32, (1, experts), 1) == place
    own_prob = jnp.sum(jnp.where(own_column, router_probs, 0.0), axis=1, keepdims=True)
    own_gate = own_prob.reshape(group, 1, rows)
    gate_slot = jnp.sum(picker.astype(F32) * own_gate, axis=2).reshape(group * capacity, 1)

    received = pick(hidden_all).astype(BF)
    gate_pre = dot(received, gate_matrix)
    up_pre = dot(received, up_matrix)
    logistic = jax.nn.sigmoid(gate_pre)
    silu = gate_pre * logistic
    slope = logistic * (1.0 + gate_pre * (1.0 - logistic))
    expert_hidden = (silu * up_pre).astype(BF)
    expert_result = dot(expert_hidden, down_matrix).astype(BF).astype(F32)
    hidden_grad = gate_slot * hidden_grad_raw
    gate_pre_grad = (hidden_grad * up_pre * slope).astype(BF)
    up_pre_grad = (hidden_grad * silu).astype(BF)
    row_grads = (dot_nt(gate_pre_grad, gate_matrix) + dot_nt(up_pre_grad, up_matrix)).astype(BF)
    grads_f32 = grads_in.astype(F32)
    gate_grad = jnp.sum(grads_f32 * expert_result, axis=1).reshape(group, capacity, 1)
    prob_grad = jnp.sum(picker.astype(F32) * gate_grad, axis=1).reshape(pack_rows, 1)
    logit_part = (
        prob_grad * own_prob * (jnp.where(own_column, 1.0, 0.0) - router_probs)
    ).astype(BF)
    choice_grad = (gate_slot * grads_f32).astype(BF)

    shared_pre = dot(hidden_all, gate_part)
    shared_lin = dot(hidden_all, up_part)
    shared_logistic = jax.nn.sigmoid(shared_pre)
    shared_silu = shared_pre * shared_logistic
    shared_slope = shared_logistic * (1.0 + shared_pre * (1.0 - shared_logistic))
    shared_hidden = (shared_silu * shared_lin).astype(BF)
    shared_pre_grad = (shared_hidden_grad * shared_lin * shared_slope).astype(BF)
    shared_lin_grad = (shared_hidden_grad * shared_silu).astype(BF)

    second_part = (
        unpick(row_grads)
        + dot_nt(shared_pre_grad, gate_part)
        + dot_nt(shared_lin_grad, up_part)
        + dot_nt(logit_part, router)
    )
    second_grad = lax.psum_scatter(
        second_part.astype(BF), "ep", scatter_dimension=0, tiled=True
    ).astype(F32)
    out_part = unpick((gate_slot * expert_result).astype(BF)) + dot(shared_hidden, down_part)
    out_sum = lax.psum_scatter(
        out_part.astype(BF), "ep", scatter_dimension=0, tiled=True
    ).astype(F32)
    layer_out = (middle + out_sum).astype(BF)

    def over_reps(term):
        return lax.psum_scatter(term.astype(BF), "rep", scatter_dimension=0, tiled=True).astype(
            F32
        )

    expert_gate_grad = over_reps(dot_tn(gate_pre_grad, received)).T[None]
    expert_up_grad = over_reps(dot_tn(up_pre_grad, received)).T[None]
    expert_down_grad = over_reps(dot_tn(choice_grad, expert_hidden)).T[None]

    gate_term = dot_tn(hidden_all, shared_pre_grad)
    up_term = dot_tn(hidden_all, shared_lin_grad)
    down_term = dot_tn(shared_hidden, grad_all)
    stacked = jnp.concatenate(
        [
            gate_term.astype(BF).reshape(reps, width // reps, ff_part),
            up_term.astype(BF).reshape(reps, width // reps, ff_part),
        ],
        axis=2,
    )
    stacked = lax.psum_scatter(stacked, "rep", scatter_dimension=0, tiled=True)
    shared_down_grad = over_reps(down_term)
    stacked = lax.all_to_all(
        stacked.reshape(group, -1, 2 * ff_part), "ep", split_axis=0, concat_axis=0, tiled=True
    ).astype(F32)

    def columns(term):
        return (
            term.reshape(group, -1, reps, ff_row).transpose(1, 2, 0, 3).reshape(-1, ff)
        )

    shared_gate_grad = columns(stacked[:, :, :ff_part])
    shared_up_grad = columns(stacked[:, :, ff_part:])

    grad_output = out_grad.astype(F32)
    grad_normed = second_grad * gain_second
    middle_grad = grad_output + scale_second * (
        grad_normed
        - normed_second * jnp.mean(grad_normed * normed_second, axis=1, keepdims=True)
    )
    gain_second_term = jnp.sum(second_grad * normed_second, axis=0)
    attn_grad = middle_grad.astype(BF)
    attended_grad = dot_nt(attn_grad, output_matrix).astype(BF)

    def over_all(term):
        columns_in = term.shape[1]
        term = term.astype(BF).reshape(reps, group, -1, columns_in).transpose(1, 0, 2, 3)
        term = lax.psum_scatter(term, "ep", scatter_dimension=0, tiled=False)
        return lax.psum_scatter(term, "rep", scatter_dimension=0, tiled=False).astype(F32)

    early = over_all(
        jnp.concatenate(
            [
                dot_tn(attended_low, attn_grad),
                dot_tn(hidden_all, logit_part),
                gain_second_term[:, None],
                jnp.zeros((width, pad - 1 - experts), F32),
            ],
            axis=1,
        )
    )

    dq, dk_win, dv_win = attend_back(
        near, queries, k_win, v_win, attended_grad, attended, lse, seg_own, seg_win, cos, sin
    )
    query_matrix = dense[:, :width]
    key_matrix = dense[:, width : 2 * width]
    value_matrix = dense[:, 2 * width : 3 * width]
    first_part = dot_nt(dk_win, key_matrix) + dot_nt(dv_win, value_matrix)
    first_own = dot_nt(dq, query_matrix)
    x_f32 = x_win.astype(F32)
    normed_win = x_f32 * rms_scale(x_f32)
    normed_first = normed_win[:rows]
    scale_first = rms_scale(layer_inputs)
    gain_first_term = jnp.sum(first_part * normed_win, axis=0) + jnp.sum(
        first_own * normed_first, axis=0
    )
    by_slot = first_part.reshape(back + 1, 2, rows, width)
    given = lax.ppermute(by_slot[:, 1].astype(BF), "ep", swap).astype(F32)
    sums = by_slot[:, 0] + given
    first_grad = sums[back]
    for k in range(back - 1, -1, -1):
        first_grad = sums[k] + lax.ppermute(first_grad.astype(BF), "ep", downward).astype(F32)
    first_grad = first_grad + first_own
    grad_normed = first_grad * gain_first
    tokens_grad = middle_grad + scale_first * (
        grad_normed - normed_first * jnp.mean(grad_normed * normed_first, axis=1, keepdims=True)
    )
    late = over_all(
        jnp.concatenate(
            [
                dot_tn(hidden_win[:rows], dq),
                dot_tn(hidden_win, dk_win),
                dot_tn(hidden_win, dv_win),
                gain_first_term[:, None],
                jnp.zeros((width, pad - 1), F32),
            ],
            axis=1,
        )
    )
    return (
        layer_out,
        tokens_grad,
        late[:, 3 * width],
        late[:, :width],
        late[:, width : 2 * width],
        late[:, 2 * width : 3 * width],
        early[:, :width],
        early[:, width + experts],
        early[:, width : width + experts],
        shared_gate_grad,
        shared_up_grad,
        shared_down_grad,
        expert_gate_grad,
        expert_up_grad,
        expert_down_grad,
    )


def solution(mesh):
    row = P(ALL, None)
    expert = P("ep", None, None)
    expert_out = P("ep", None, "rep")
    return jax.shard_map(
        shards,
        mesh=mesh,
        in_specs=(
            row,
            P("rep", "ep"),
            row,
            P(ALL),
            row,
            row,
            row,
            row,
            P(ALL),
            row,
            row,
            row,
            row,
            expert,
            expert,
            expert,
            row,
        ),
        out_specs=(
            row,
            row,
            P(ALL),
            row,
            row,
            row,
            row,
            P(ALL),
            row,
            row,
            row,
            row,
            expert_out,
            expert_out,
            expert_out,
        ),
        check_vma=False,
    )
```
